32 devices in a mesh: grp: 2 (over y), theta: 8 (over z, x), phi: 2 (over core).
Axes of the slice: x: 2, y: 2, z: 4, core: 2. Of those that a mesh axis runs over, the one named last changes fastest.
Arguments:
- maps: bfloat16 [8, 4096, 4096], P('grp', 'theta', 'phi'), parts along dimension 0, may hold values from -6 to 6
- deltas: bfloat16 [4096, 4, 4096], P('phi', None, 'theta'), may hold values from -1 to 1
- spin_rows: bfloat16 [4096, 2, 4], P('phi'), may hold values from -1 to 1
- ell_index: int32 [4], replicated, may hold values from 1024 to 2047
- owner_map: int32 [4096], replicated, may hold values from 0 to 4095, each once
- prior: float32 [4], replicated, may hold values from 0.3 to 3
Outputs:
- gradient: float32 [8, 2, 4096], P('grp', None, ('theta', 'phi')), parts along dimension 0
The draws below stay inside these ranges and needn't reach their ends.
There are 2 independent parts, one for each index of `grp`. The reference program is written for one: setup_inputs(seed, part) draws one part's arguments, and reference() takes and returns one part's arrays. A program takes and returns all parts, laid end to end along the dimension named above; an argument that names none is the same for every part. Nothing has to cross between parts.
Inputs may be any that keep to these rules, and one draw needn't show every extreme that they name: `ell_index`: every selected degree is at least 1024; tables may repeat a degree. A permutation of the Fourier indices; slot s of deltas and of the output belongs to the frequency owner_map[s].
All inputs are finite; a program needn't handle non-finite values.
Results may differ from the reference program's by a relative error of at most 0.0003.
Values may be sent and summed in bfloat16 or wider, within the bound.
No kernel may reach another device: no remote copies, remote signals or barrier semaphores. Data moves between devices by JAX's collectives and lax.ppermute only.
A program may use at most 256 MiB of HBM per device.

```python
import math
import jax
import jax.numpy as jnp
from jax import lax

L = 2048
NL = 4


def touch_ends(result, rng, low, top_value):
    place = [jax.random.randint(jax.random.fold_in(rng, axis), (), 0, length) for axis, length in enumerate(result.shape)]
    longest = result.shape.index(max(result.shape))
    beside = place[:longest] + [(place[longest] + 1) % result.shape[longest]] + place[longest + 1:]
    return result.at[tuple(place)].set(low).at[tuple(beside)].set(top_value)


def shard_levels(rng, dims, shards, low, high):
    factor_of, own = 1.0, jax.random.fold_in(rng, 6)
    for dim, parts in shards:
        steps = jnp.exp(jax.random.uniform(jax.random.fold_in(own, dim), (parts,), jnp.float32, low / len(shards), high / len(shards)))
        factor_of = factor_of * jnp.repeat(steps, dims[dim] // parts).reshape([-1 if axis == dim else 1 for axis in range(len(dims))])
    return factor_of


def bell_draw(rng, dims, width, limit, pieces=(), kind=jnp.bfloat16):
    array = width * jax.random.normal(rng, dims, jnp.float32)
    if pieces:
        array = array * shard_levels(rng, dims, pieces, -0.22, 0.18)
    return jnp.clip(array, -limit, limit).astype(kind)


def setup_inputs(seed: int = 0, part: int = 0) -> dict:
    streams_of = jax.random.split(jax.random.key(seed), 7)
    part_keys = jax.random.split(jax.random.fold_in(streams_of[6], part), 7)
    maps = bell_draw(part_keys[0], (4, 2 * L, 2 * L), 1.0, 6.0, ((1, 8), (2, 2)))
    deltas = jnp.clip(jax.random.uniform(streams_of[1], (2 * L, NL, 2 * L), jnp.float32, -1.0, 1.0) * shard_levels(streams_of[1], (2 * L, NL, 2 * L), ((0, 2), (2, 8)), -0.4, 0.0), -1.0, 1.0).astype(jnp.bfloat16)
    spin_rows = jnp.clip(jax.random.uniform(streams_of[2], (2 * L, 2, NL), jnp.float32, -1.0, 1.0) * shard_levels(streams_of[2], (2 * L, 2, NL), ((0, 2),), -0.4, 0.0), -1.0, 1.0).astype(jnp.bfloat16)
    ell_index = touch_ends(jax.random.randint(streams_of[3], (NL,), L // 2, L), jax.random.fold_in(streams_of[3], 1), L // 2, L - 1).astype(jnp.int32)
    owner_map = jax.random.permutation(streams_of[4], 2 * L).astype(jnp.int32)
    prior = jnp.clip(jnp.exp(jax.random.uniform(streams_of[5], (NL,), jnp.float32, math.log(0.3), math.log(3.0))), 0.3, 3.0)
    return dict(maps=maps, deltas=deltas, spin_rows=spin_rows, ell_index=ell_index, owner_map=owner_map, prior=prior)


def signed_freq(length):
    positions = jnp.arange(length, dtype=jnp.int32)
    return jnp.where(positions < length // 2, positions, positions - length)

def reference(maps, deltas, spin_rows, ell_index, owner_map, prior):
    length = 2 * L
    values = maps.astype(jnp.float32)
    prod_real = values[1] * values[2]
    prod_imag = values[1] * values[3]
    scalar_spec = jnp.fft.fft2(values[0]) / length
    spin_spec = jnp.fft.fft2(lax.complex(prod_real, prod_imag)) / length
    planes = [jnp.real(scalar_spec)[:, owner_map].astype(jnp.float32), jnp.imag(scalar_spec)[:, owner_map].astype(jnp.float32), jnp.real(spin_spec)[:, owner_map].astype(jnp.float32), jnp.imag(spin_spec)[:, owner_map].astype(jnp.float32)]
    freq = signed_freq(length)
    slot_freq = freq[owner_map]
    turns = jnp.mod(-slot_freq, 4)
    phase_real = jnp.where(turns == 0, 1.0, jnp.where(turns == 2, -1.0, 0.0)).astype(jnp.float32)
    phase_imag = jnp.where(turns == 1, 1.0, jnp.where(turns == 3, -1.0, 0.0)).astype(jnp.float32)
    outputs = []
    for degree in range(NL):
        ell = ell_index[degree]
        ell_float = ell.astype(jnp.float32)
        keep_rows = (jnp.abs(freq) <= ell).astype(jnp.float32)
        keep_slots = (jnp.abs(slot_freq) <= ell).astype(jnp.float32)
        table = deltas[:, degree, :].astype(jnp.float32)
        weight = 2.0 * math.pi / length * jnp.sqrt((2.0 * ell_float + 1.0) / (4.0 * math.pi))
        sums = []
        for plane_pos in range(4):
            spin = plane_pos // 2
            row_weights = spin_rows[:, spin, degree].astype(jnp.float32) * keep_rows
            total = jnp.einsum('k,ks->s', row_weights, table * planes[plane_pos], precision=lax.Precision.HIGHEST)
            sums.append(total * weight * keep_slots)
        coupling = prior[degree] * jnp.sqrt(ell_float * (ell_float + 1.0)) / L
        inner_real = -sums[3] - coupling * sums[0]
        inner_imag = sums[2] - coupling * sums[1]
        out_real = phase_real * inner_real - phase_imag * inner_imag
        out_imag = phase_real * inner_imag + phase_imag * inner_real
        outputs.append(jnp.stack([out_real, out_imag]))
    return jnp.stack(outputs)
```

```python
import functools
import math

import jax
import jax.numpy as jnp
import numpy as np
from jax import lax
from jax.experimental import pallas as pl
from jax.experimental.pallas import tpu as pltpu
from jax.sharding import PartitionSpec as P

RADIX = 16
LINK_SCALE = 0.25
LINK_TYPE = jnp.float16
VMEM_BYTES = 56 * 1024 * 1024


def add(x, y):
    return y if x is None else x if y is None else x + y


def sub(x, y):
    return x if y is None else -y if x is None else x - y


def dft4(x0, x1, x2, x3):
    s02 = (add(x0[0], x2[0]), add(x0[1], x2[1]))
    d02 = (sub(x0[0], x2[0]), sub(x0[1], x2[1]))
    s13 = (add(x1[0], x3[0]), add(x1[1], x3[1]))
    d13 = (sub(x1[0], x3[0]), sub(x1[1], x3[1]))
    return (
        (add(s02[0], s13[0]), add(s02[1], s13[1])),
        (add(d02[0], d13[1]), sub(d02[1], d13[0])),
        (sub(s02[0], s13[0]), sub(s02[1], s13[1])),
        (sub(d02[0], d13[1]), add(d02[1], d13[0])),
    )


def turn(x, power):
    re, im = x
    if power == 0:
        return x
    if power == 4:
        return (im, None if re is None else -re)
    c = math.cos(2 * math.pi * power / RADIX)
    s = math.sin(2 * math.pi * power / RADIX)
    if im is None:
        return (re * c, re * (-s))
    if re is None:
        return (im * s, im * c)
    return (re * c + im * s, im * c - re * s)


def dft16(xs):
    inner = [dft4(xs[a], xs[a + 4], xs[a + 8], xs[a + 12]) for a in range(4)]
    out = [None] * RADIX
    for low in range(4):
        turned = [turn(inner[a][low], a * low) for a in range(4)]
        for high, value in enumerate(dft4(*turned)):
            out[low + 4 * high] = value
    return out


def split_store(hi_ref, lo_ref, k, rows, lanes, value):
    hi = value.astype(jnp.bfloat16)
    hi_ref[k, rows, lanes] = hi
    lo_ref[k, rows, lanes] = (value - hi.astype(jnp.float32)).astype(jnp.bfloat16)


def first_stage(load, turn_ref, hi_ref, lo_ref, row_total, inner):
    step = 16
    width = min(128, inner)

    def body(i, carry):
        rows = pl.ds(pl.multiple_of(i * step, step), step)
        for lane in range(0, inner, width):
            xs = [load(a, rows, lane, width) for a in range(RADIX)]
            ys = dft16(xs)
            for k in range(RADIX):
                re, im = ys[k]
                if k:
                    c = turn_ref[0, k : k + 1, lane : lane + width]
                    s = turn_ref[1, k : k + 1, lane : lane + width]
                    if im is None:
                        re, im = re * c, -re * s
                    else:
                        re, im = re * c + im * s, im * c - re * s
                if im is None:
                    im = jnp.zeros_like(re)
                split_store(hi_ref, lo_ref, k, rows, pl.ds(lane, width), re)
                split_store(hi_ref, lo_ref, k, rows, pl.ds(inner + lane, width), im)
        return carry

    lax.fori_loop(0, row_total // step, body, 0)


def second_stage(k, w_ref, hi_ref, lo_ref):
    dims = (((1,), (1,)), ((), ()))
    hi = hi_ref[k]
    lo = lo_ref[k]
    dot = functools.partial(lax.dot_general, dimension_numbers=dims, preferred_element_type=jnp.float32)
    return dot(w_ref[0], hi) + dot(w_ref[0], lo) + dot(w_ref[1], hi)


def front_kernel(rows_ref, w_ref, turn_ref, *refs, spin):
    planes = refs[: 3 if spin else 1]
    out_ref, hi_ref, lo_ref, spec_ref = refs[len(planes) :]
    halves, _, row_total, _ = planes[0].shape
    inner = w_ref.shape[1] // 2
    per_half = RADIX // halves

    def load(a, rows, lane, width):
        half, start = a // per_half, (a % per_half) * inner + lane
        read = lambda plane: planes[plane][half, 0, rows, pl.ds(start, width)].astype(jnp.float32)
        if not spin:
            return (read(0), None)
        base = read(0)
        return (base * read(1), base * read(2))

    first_stage(load, turn_ref, hi_ref, lo_ref, row_total, inner)

    def body(k, carry):
        g = second_stage(k, w_ref, hi_ref, lo_ref)
        start = pl.multiple_of(k * inner, inner)
        spec_ref[pl.ds(start, inner), :row_total] = g[:inner] * LINK_SCALE
        spec_ref[pl.ds(start, inner), row_total:] = g[inner:] * LINK_SCALE
        return carry

    lax.fori_loop(0, RADIX, body, 0)

    def gather(i, carry):
        base = pl.multiple_of(i * 16, 16)
        for u in range(16):
            out_ref[pl.ds(base + u, 1), :] = spec_ref[pl.ds(rows_ref[base + u], 1), :]
        return carry

    lax.fori_loop(0, out_ref.shape[0] // 16, gather, 0)


def front(maps, w, turns, source_rows, spin):
    halves, _, row_total, half_cols = maps.shape
    picks = (1, 2, 3) if spin else (0,)
    inner = w.shape[1] // 2
    length = RADIX * inner
    vmem = pl.BlockSpec(memory_space=pltpu.VMEM)
    plane_specs = [
        pl.BlockSpec((halves, 1, row_total, half_cols), functools.partial(lambda p, i: (0, p, 0, 0), p))
        for p in picks
    ]
    return pl.pallas_call(
        functools.partial(front_kernel, spin=spin),
        grid=(1,),
        in_specs=[pl.BlockSpec(memory_space=pltpu.SMEM), vmem, vmem, *plane_specs],
        out_specs=vmem,
        out_shape=jax.ShapeDtypeStruct((length, 2 * row_total), jnp.float32),
        scratch_shapes=[
            pltpu.VMEM((RADIX, row_total, 2 * inner), jnp.bfloat16),
            pltpu.VMEM((RADIX, row_total, 2 * inner), jnp.bfloat16),
            pltpu.VMEM((length, 2 * row_total), jnp.float32),
        ],
        compiler_params=pltpu.CompilerParams(vmem_limit_bytes=VMEM_BYTES),
    )(source_rows, w, turns, *([maps] * len(picks)))


def back_kernel(code_ref, w_ref, turn_ref, weight_ref, table_ref, out_ref, hi_ref, lo_ref, g_ref):
    slots = code_ref.shape[1]
    inner = w_ref.shape[1] // 2
    parts, degrees, _, part_rows, _ = table_ref.shape
    step = pl.program_id(0)

    @pl.when(step == 0)
    def _():
        def load(a, rows, lane, width):
            read = lambda start: code_ref[a, rows, pl.ds(start, width)].astype(jnp.float32)
            return (read(lane), read(inner + lane))

        first_stage(load, turn_ref, hi_ref, lo_ref, slots, inner)
        out_ref[...] = jnp.zeros_like(out_ref)

    g_ref[...] = second_stage(step, w_ref, hi_ref, lo_ref)
    width = min(128, slots)
    lanes = [pl.ds(lane, width) for lane in range(0, slots, width)]
    keys = [(j, part, at) for at in range(len(lanes)) for j in range(degrees) for part in range(2)]

    def body(i, sums):
        new = dict(zip(keys, sums))
        for source in range(parts):
            local = pl.multiple_of(i * 16, 16)
            rows = pl.multiple_of(source * part_rows + i * 16, 16)
            scale = [weight_ref[0, pl.ds(rows, 16), j : j + 1] for j in range(degrees)]
            for at in range(len(lanes)):
                g = [g_ref[pl.ds(part * inner + rows, 16), lanes[at]] for part in range(2)]
                for j in range(degrees):
                    scaled = table_ref[source, j, 0, pl.ds(local, 16), lanes[at]].astype(jnp.float32) * scale[j]
                    for part in range(2):
                        product = scaled * g[part]
                        new[j, part, at] += product[:8] + product[8:]
        return tuple(new[key] for key in keys)

    sums = tuple(out_ref[j, part, :, lanes[at]] for j, part, at in keys)
    sums = lax.fori_loop(0, part_rows // 16, body, sums, unroll=True)
    for key, total in zip(keys, sums):
        out_ref[key[0], key[1], :, lanes[key[2]]] = total


def back(code, w, turns, weights, tables):
    slots = code.shape[1]
    inner = w.shape[1] // 2
    parts, degrees = tables.shape[:2]
    vmem = pl.BlockSpec(memory_space=pltpu.VMEM)
    sums = pl.pallas_call(
        back_kernel,
        grid=(RADIX,),
        in_specs=[
            vmem,
            vmem,
            vmem,
            pl.BlockSpec((1, inner, degrees), lambda k: (k, 0, 0)),
            pl.BlockSpec((parts, degrees, 1, inner // parts, slots), lambda k: (0, 0, k, 0, 0)),
        ],
        out_specs=pl.BlockSpec((degrees, 2, 8, slots), lambda k: (0, 0, 0, 0)),
        out_shape=jax.ShapeDtypeStruct((degrees, 2, 8, slots), jnp.float32),
        scratch_shapes=[
            pltpu.VMEM((RADIX, slots, 2 * inner), jnp.bfloat16),
            pltpu.VMEM((RADIX, slots, 2 * inner), jnp.bfloat16),
            pltpu.VMEM((2 * inner, slots), jnp.float32),
        ],
        compiler_params=pltpu.CompilerParams(
            vmem_limit_bytes=VMEM_BYTES, dimension_semantics=("arbitrary",)
        ),
    )(code, w, turns, weights, tables)
    return jnp.sum(sums, axis=2)


def dft_tables(length):
    inner = length // RADIX
    place = np.arange(inner)
    angle = 2 * np.pi / inner * (place[:, None] * place[None, :] % inner)
    c, s = np.cos(angle), np.sin(angle)
    full = np.block([[c, s], [-s, c]]).astype(np.float32)
    hi = full.astype(jnp.bfloat16)
    lo = (full - hi.astype(np.float32)).astype(jnp.bfloat16)
    twist = 2 * np.pi / length * (np.arange(RADIX)[:, None] * place[None, :])
    return (
        jnp.asarray(np.stack([hi, lo])),
        jnp.asarray(np.stack([np.cos(twist), np.sin(twist)]).astype(np.float32)),
    )


def on_device(maps, deltas, spin_rows, ell_index, owner_map, prior):
    axes = ("theta", "phi")
    phi_count = lax.axis_size("phi")
    ranks = lax.axis_size("theta") * phi_count
    planes, block_rows, half_cols = maps.shape
    length = half_cols * phi_count
    inner = length // RADIX
    rows = block_rows // phi_count
    slots = length // ranks
    degrees = deltas.shape[1]
    w, turns = dft_tables(length)

    halves = lax.all_to_all(
        maps.reshape(planes, phi_count, rows, half_cols).transpose(1, 0, 2, 3),
        "phi",
        split_axis=0,
        concat_axis=0,
    )
    source_rows = jnp.mod(owner_map, RADIX) * inner + owner_map // RADIX
    received = []
    for spin in range(2):
        code = front(halves, w, turns, source_rows, spin)
        if spin == 1:
            code, deltas = lax.optimization_barrier((code, deltas))
        code = lax.all_to_all(code.reshape(ranks, slots, 2 * rows).astype(LINK_TYPE), axes, split_axis=0, concat_axis=0)
        code = code.astype(jnp.float32).reshape(RADIX, ranks // RADIX, slots, 2, rows)
        received.append(code.transpose(0, 2, 3, 1, 4).reshape(RADIX, slots, 2 * inner))

    part = inner // phi_count
    tables = deltas.reshape(part, RADIX, degrees, phi_count, slots).transpose(3, 2, 1, 0, 4)
    tables = lax.all_to_all(tables, "phi", split_axis=0, concat_axis=0)
    spin_all = lax.all_gather(spin_rows, "phi", axis=0, tiled=True).astype(jnp.float32)
    positions = jnp.arange(length, dtype=jnp.int32)
    freq = jnp.where(positions < length // 2, positions, positions - length)
    keep_rows = (jnp.abs(freq)[:, None] <= ell_index[None, :]).astype(jnp.float32)
    shares = []
    for spin in range(2):
        weights = (spin_all[:, spin] * keep_rows).reshape(inner, RADIX, degrees).transpose(1, 0, 2)
        shares.append(back(received[spin], w, turns, weights, tables))

    slot_start = (lax.axis_index("theta") * phi_count + lax.axis_index("phi")) * slots
    share_ids = lax.dynamic_slice_in_dim(owner_map, slot_start, slots)
    slot_freq = jnp.where(share_ids < length // 2, share_ids, share_ids - length)
    ell_float = ell_index.astype(jnp.float32)
    weight = 2.0 * math.pi / length * jnp.sqrt((2.0 * ell_float + 1.0) / (4.0 * math.pi)) / (length * LINK_SCALE)
    keep_slots = (jnp.abs(slot_freq)[None, :] <= ell_index[:, None]).astype(jnp.float32) * weight[
        :, None
    ]
    scalar_real = shares[0][:, 0] * keep_slots
    scalar_imag = shares[0][:, 1] * keep_slots
    spin_real = shares[1][:, 0] * keep_slots
    spin_imag = shares[1][:, 1] * keep_slots
    coupling = (prior * jnp.sqrt(ell_float * (ell_float + 1.0)) / (length // 2))[:, None]
    inner_real = -spin_imag - coupling * scalar_real
    inner_imag = spin_real - coupling * scalar_imag
    turned = jnp.mod(-slot_freq, 4)
    phase_real = jnp.where(turned == 0, 1.0, jnp.where(turned == 2, -1.0, 0.0)).astype(jnp.float32)
    phase_imag = jnp.where(turned == 1, 1.0, jnp.where(turned == 3, -1.0, 0.0)).astype(jnp.float32)
    out_real = phase_real * inner_real - phase_imag * inner_imag
    out_imag = phase_real * inner_imag + phase_imag * inner_real
    return jnp.stack([out_real, out_imag], axis=1)


def solution(mesh):
    placed = (
        P("grp", "theta", "phi"),
        P("phi", None, "theta"),
        P("phi", None, None),
        P(),
        P(),
        P(),
    )
    return jax.shard_map(
        on_device,
        mesh=mesh,
        in_specs=placed,
        out_specs=P("grp", None, ("theta", "phi")),
        check_vma=False,
    )
```
